128 devices in a mesh: band: 16 (over x, y), grp: 8 (over z, core).
Axes of the slice: x: 4, y: 4, z: 4, core: 2. Of those that a mesh axis runs over, the one named last changes fastest.
Arguments:
- spectral: bfloat16 [640, 2, 4, 16, 640], P(('band', 'grp')), may hold values from -6 to 6
- legendre: bfloat16 [640, 640, 640], P(('band', 'grp')), may hold values from -4 to 4
- owner_table: int32 [640], replicated, may hold values from 0 to 639, as said below
Outputs:
- spectral_out: float32 [640, 2, 4, 16, 640], P(('band', 'grp'))
The draws below stay inside these ranges and needn't reach their ends.
Inputs may be any that keep to these rules, and one draw needn't show every extreme that they name: `owner_table`: A permutation of the zonal wavenumbers. Slot s of the whole array belongs to device s // 5 along band+grp. For each q below 2, slots 2q and 2q + 1 of every device hold wavenumbers whose sum is (4q + 2) * 128 - 1.
All inputs are finite; a program needn't handle non-finite values.
Results may differ from the reference program's by a relative error of at most 0.0067.
Values may be sent and summed in bfloat16 or wider, within the bound.
A program may use at most 64 MiB of HBM per device.

```python
import math
import jax
import jax.numpy as jnp
from jax import lax

M = 640
N = 640
NLAT = 1280
NLON = 2560
FIELDS = 4
LEV = 16
MDEV = 5
NHALF = 640


def draw_owner_table(key, part):
    device_count = M // MDEV
    columns = []
    shuffled = None
    for row_number in range(MDEV):
        if row_number % 2 == 1:
            columns.append(row_number * device_count + device_count - 1 - shuffled)
        else:
            shuffled = jax.random.permutation(jax.random.fold_in(key, row_number + 17), device_count)
            columns.append(row_number * device_count + shuffled)
    return jnp.stack(columns, axis=1).reshape(M).astype(jnp.int32)


def level_of(own_key, shape, split, least, top_value):
    level, own = 1.0, jax.random.fold_in(own_key, 6)
    for position, blocks in split:
        heights = jnp.exp(jax.random.uniform(jax.random.fold_in(own, position), (blocks,), jnp.float32, least / len(split), top_value / len(split)))
        level = level * jnp.repeat(heights, shape[position] // blocks).reshape([-1 if axis == position else 1 for axis in range(len(shape))])
    return level


def gaussian(key, dims, spread, bound, split=(), held_as=jnp.bfloat16):
    loudness = level_of(key, dims, split, -0.22, 0.18) if split else 1.0
    drawn = jax.random.normal(key, dims, jnp.float32) * spread * loudness
    return jnp.minimum(jnp.maximum(drawn, -bound), bound).astype(held_as)


def setup_inputs(seed: int = 0) -> dict:
    keys = jax.random.split(jax.random.key(seed), 4)
    spectral = gaussian(keys[0], (M, 2, FIELDS, LEV, N), 1.0, 6.0, ((0, 128),))
    legendre = gaussian(keys[1], (M, N, NHALF), 1.0, 4.0, ((0, 128),))
    owner_table = draw_owner_table(jax.random.fold_in(keys[3], 71), 0)
    return {"spectral": spectral, "legendre": legendre, "owner_table": owner_table}


def parity_sign(wavenumber, length):
    degree_index = jnp.arange(length, dtype=jnp.int32)
    odd_part = (degree_index[None, :] - wavenumber[:, None]) % 2
    return (1 - 2 * odd_part).astype(jnp.float32)

def make_trig(wavenumber):
    lon_index = jnp.arange(NLON, dtype=jnp.int32)
    phases = wavenumber[:, None] * lon_index[None, :] % NLON
    angles = phases.astype(jnp.float32) * (2.0 * math.pi / NLON)
    return jnp.stack([jnp.cos(angles), -jnp.sin(angles)], axis=1).astype(jnp.bfloat16)

def reference(spectral, legendre, owner_table):
    highest = lax.Precision.HIGHEST
    wavenumber = owner_table.astype(jnp.int32)
    degree_index = jnp.arange(N, dtype=jnp.int32)
    keep_mask = (degree_index[None, :] >= wavenumber[:, None]).astype(jnp.float32)
    parity = parity_sign(wavenumber, N)
    row_total = 2 * FIELDS * LEV

    def inverse_one(packed):
        spec_slot, table_slot, keep_slot, sign_slot = packed
        flattened = spec_slot.astype(jnp.float32).reshape(row_total, N) * keep_slot[None, :]
        table_wide = table_slot.astype(jnp.float32)
        northern = jnp.dot(flattened, table_wide, precision=highest)
        mirrored = jnp.dot(flattened * sign_slot[None, :], table_wide, precision=highest)
        combined = jnp.concatenate([northern, jnp.flip(mirrored, axis=1)], axis=1)
        return (combined * (1.0 / math.sqrt(N))).astype(jnp.bfloat16).reshape(2, FIELDS, LEV, NLAT)
    fourier = lax.map(inverse_one, (spectral, legendre, keep_mask, parity))
    trig_wide = make_trig(wavenumber).astype(jnp.float32)

    def grid_level(level_fourier):
        grid_values = jnp.einsum('scfi,scl->fil', level_fourier.astype(jnp.float32), trig_wide, precision=highest)
        grid_values = grid_values * (1.0 / math.sqrt(M))
        product = (grid_values * jnp.roll(grid_values, -1, axis=0)).astype(jnp.bfloat16)
        product = lax.optimization_barrier(product).astype(jnp.float32)
        zonal_coeffs = jnp.einsum('fil,scl->scfi', product, trig_wide, precision=highest)
        return (zonal_coeffs * (2.0 / math.sqrt(NLON))).astype(jnp.bfloat16)
    zonal_coeffs = lax.map(grid_level, jnp.moveaxis(fourier, 3, 0))
    zonal_coeffs = jnp.moveaxis(zonal_coeffs, 0, 3)

    def direct_one(packed):
        zonal_slot, table_slot, keep_slot, sign_slot = packed
        values = zonal_slot.astype(jnp.float32).reshape(row_total, NLAT)
        northern = values[:, :NHALF]
        mirrored = jnp.flip(values[:, NHALF:], axis=1)
        plus_part = lax.optimization_barrier((northern + mirrored).astype(jnp.bfloat16)).astype(jnp.float32)
        minus_part = lax.optimization_barrier((northern - mirrored).astype(jnp.bfloat16)).astype(jnp.float32)
        table_wide = table_slot.astype(jnp.float32)
        out_plus = jnp.dot(plus_part, table_wide.T, precision=highest)
        out_minus = jnp.dot(minus_part, table_wide.T, precision=highest)
        chosen = jnp.where(sign_slot[None, :] > 0, out_plus, out_minus)
        chosen = chosen * keep_slot[None, :] * (1.0 / math.sqrt(NLAT))
        return chosen.reshape(2, FIELDS, LEV, N)
    return lax.map(direct_one, (zonal_coeffs, legendre, keep_mask, parity))
```

```python
import functools
import math

import jax
import jax.numpy as jnp
from jax import lax
from jax.experimental import pallas as pl
from jax.experimental.pallas import tpu as pltpu
from jax.sharding import PartitionSpec as P

M = 640
N = 640
NLAT = 1280
NLON = 2560
FIELDS = 4
LEV = 16
SLOTS = 5
BAND = 16
GRP = 8
DEV = BAND * GRP
ROWS = 2 * FIELDS * LEV
MESH = pl.DeviceIdType.MESH
F32 = jnp.float32
BF16 = jnp.bfloat16
GROUPS = ((0, 3), (3, 5))
NT = (((1,), (1,)), ((), ()))


def dot(a, b):
    return jnp.dot(a, b, preferred_element_type=F32)


def iota(shape, axis):
    return lax.broadcasted_iota(jnp.int32, shape, axis)


def turned_cos(turns, quarter):
    whole = jnp.floor(turns * (4.0 / NLON) + 0.5)
    x = (turns - whole * (NLON / 4.0)) * (2.0 * math.pi / NLON)
    y = x * x
    cosine = 1.0 + y * (-0.5 + y * (1.0 / 24 + y * (-1.0 / 720 + y * (1.0 / 40320))))
    sine = x * (1.0 + y * (-1.0 / 6 + y * (1.0 / 120 + y * (-1.0 / 5040 + y * (1.0 / 362880)))))
    k = whole + quarter
    k = k - 4.0 * jnp.floor(k * 0.25)
    odd = (k == 1.0) | (k == 3.0)
    value = jnp.where(odd, sine, cosine)
    return jnp.where((k == 1.0) | (k == 2.0), -value, value)


def pair_rows(x):
    return x.reshape(x.shape[0] // 2, 2, 128)


def flat_rows(x):
    return x.reshape(-1, 128)


def kernel(
    tab_smem, tab_ref, spec_hbm, leg_hbm, out_hbm,
    spec_v, leg_v, x_v, send_q, send_f, grid_q, grid_f, tt, tr, prod_q, prod_f,
    back_q, back_f, home_q, home_f, out_v,
    in_sem, out_sem, own_sem, ssem, rsem, plane_sem,
):
    b0 = lax.axis_index("band")
    g0 = lax.axis_index("grp")
    me = b0 * GRP + g0

    barrier = pltpu.get_barrier_semaphore()
    for i in range(1, BAND):
        pl.semaphore_signal(barrier, inc=1, device_id=((b0 + i) & (BAND - 1), g0), device_id_type=MESH)
    for i in range(1, GRP):
        pl.semaphore_signal(barrier, inc=1, device_id=(b0, (g0 + i) & (GRP - 1)), device_id_type=MESH)

    get_spec = pltpu.make_async_copy(spec_hbm, spec_v, in_sem.at[0])
    get_rem = pltpu.make_async_copy(leg_hbm.at[:, :, pl.ds(512, 128)], leg_v.at[:, :, pl.ds(512, 128)], in_sem.at[1])
    get_main = pltpu.make_async_copy(leg_hbm.at[:, :, pl.ds(0, 512)], leg_v.at[:, :, pl.ds(0, 512)], in_sem.at[2])
    get_spec.start()
    get_rem.start()
    get_main.start()

    degree = iota((1, N), 1)
    waves = [tab_smem[me * SLOTS + s] for s in range(SLOTS)]

    r = iota((ROWS, ROWS), 0)
    perm = jnp.where(iota((ROWS, ROWS), 1) == (r & 1) * 64 + (r >> 1), 1.0, 0.0).astype(BF16)
    get_spec.wait()
    for s in range(SLOTS):
        rows = dot(perm, spec_v[s])
        rows = jnp.where(degree >= waves[s], rows, 0.0)
        flip = jnp.where(((degree - waves[s]) & 1) == 1, -1.0, 1.0)
        x_v[s, :ROWS] = rows.astype(BF16)
        x_v[s, ROWS:] = (rows * flip).astype(BF16)

    pl.semaphore_wait(barrier, BAND - 1 + GRP - 1)
    for i in range(1, GRP):
        pl.semaphore_signal(plane_sem, inc=1, device_id=(b0, (g0 + i) & (GRP - 1)), device_id_type=MESH)

    scale_in = 1.0 / math.sqrt(N)
    lane_group = iota((32, 128), 1) >> 5
    get_rem.wait()
    for s in range(SLOTS):
        part = dot(x_v[s], leg_v[s, :, 512:640]) * scale_in
        for h in range(2):
            fields = [part[h * 128 + 32 * f : h * 128 + 32 * f + 32] for f in range(FIELDS)]
            for q in range(4):
                moved = [pltpu.roll(fields[f], (32 * (f - q)) % 128, 1) if f != q else fields[f] for f in range(FIELDS)]
                both = jnp.where(
                    lane_group < 2,
                    jnp.where(lane_group == 0, moved[0], moved[1]),
                    jnp.where(lane_group == 2, moved[2], moved[3]),
                )
                send_q[s, h * 4 + q] = pair_rows(both.astype(BF16))

    pl.semaphore_wait(plane_sem, GRP - 1)

    x0, y0, z0, c0 = b0 >> 2, b0 & 3, g0 >> 1, g0 & 1

    def peer(t):
        turn = t >> 1
        dx = turn & 3
        dy = ((turn >> 2) + turn) & 3
        dz = ((turn >> 4) + turn) & 3
        b = (((x0 + dx) & 3) << 2) + ((y0 + dy) & 3)
        g = (((z0 + dz) & 3) << 1) + ((c0 + t) & 1)
        return b, g

    def exchange(piece, source, target, which):
        def step(t, carry):
            b, g = peer(t)
            pltpu.make_async_remote_copy(
                src_ref=source(b, g), dst_ref=target, send_sem=ssem.at[which], recv_sem=rsem.at[which],
                device_id=(b, g), device_id_type=MESH,
            ).start()
            return carry

        lax.fori_loop(1, DEV, step, 0)
        own = pltpu.make_async_copy(source(b0, g0), target, own_sem.at[which])
        own.start()
        every = pltpu.make_async_remote_copy(
            src_ref=piece, dst_ref=piece, send_sem=ssem.at[which], recv_sem=rsem.at[which],
            device_id=(b0, g0), device_id_type=MESH,
        )
        return own, every

    def arrived(handle):
        handle[0].wait()
        handle[1].wait_recv()

    out_q = exchange(grid_q.at[:, pl.ds(0, DEV - 1)], lambda b, g: send_q.at[:, g, b], grid_q.at[:, me], 0)

    get_main.wait()

    def inverse(s, carry):
        part = dot(x_v[s], leg_v[s, :, 0:512]) * scale_in
        for h in range(2):
            for blk in range(4):
                piece = part[h * 128 : h * 128 + 128, blk * 128 : blk * 128 + 128].astype(BF16)
                send_f[s, h * 4 + blk] = piece.reshape(FIELDS, LEV, 2, 128)
        return carry

    lax.fori_loop(0, SLOTS, inverse, 0)
    out_f = exchange(grid_f.at[:, :, pl.ds(0, DEV - 1)], lambda b, g: send_f.at[:, g, :, b], grid_f.at[:, :, me], 1)

    tab = tab_ref[...].astype(F32)
    high = jnp.floor(tab * (1.0 / 32))
    low = tab - 32.0 * high
    row8 = iota((8, M), 0)
    split_rows = jnp.where(row8 == 0, high, jnp.where(row8 == 1, low, 0.0)).astype(BF16)
    high_rows = jnp.broadcast_to(high, (128, M)).astype(BF16)
    low_rows = jnp.broadcast_to(low, (128, M)).astype(BF16)

    def tables(s, carry):
        column = iota((M, 256), 0)
        pick = jnp.where(column == (iota((M, 256), 1) >> 1) * SLOTS + s, 1.0, 0.0).astype(BF16)
        found = dot(split_rows, pick)
        wave = found[0:1] * 32.0 + found[1:2]
        quarter = (iota((1, 256), 1) & 1).astype(F32)
        turn = 2.0 * turned_cos(wave * 128.0, 0.0)
        at = pl.multiple_of(s * 256, 256)

        def strip_tt(i, carry):
            line = (iota((32, 256), 0) + i * 32).astype(F32)
            last = turned_cos(wave * line, quarter)
            value = turned_cos(wave * (line + 128.0), quarter)
            tt[pl.ds(pl.multiple_of(i * 32, 32), 32), pl.ds(at, 256)] = last.astype(BF16)
            for a in range(1, NLON // 128):
                tt[pl.ds(pl.multiple_of(a * 128 + i * 32, 32), 32), pl.ds(at, 256)] = value.astype(BF16)
                value, last = turn * value - last, value
            return carry

        lax.fori_loop(0, 4, strip_tt, 0)

        lane = iota((256, M), 1)
        pick_rows = jnp.where(lane == (iota((256, M), 0) >> 1) * SLOTS + s, 1.0, 0.0).astype(BF16)
        wave_rows = 32.0 * lax.dot_general(pick_rows, high_rows, NT, preferred_element_type=F32)
        wave_rows = wave_rows + lax.dot_general(pick_rows, low_rows, NT, preferred_element_type=F32)
        for i in range(4):
            w = wave_rows[i * 64 : i * 64 + 64]
            line = iota((64, 128), 1).astype(F32)
            quarter = (iota((64, 128), 0) & 1).astype(F32)
            turn = 2.0 * turned_cos(w * 128.0, 0.0)
            last = turned_cos(w * line, quarter)
            value = turned_cos(w * (line + 128.0), quarter)
            tr[pl.ds(at + i * 64, 64), 0:128] = last.astype(BF16)
            for a in range(1, NLON // 128):
                tr[pl.ds(at + i * 64, 64), a * 128 : a * 128 + 128] = value.astype(BF16)
                value, last = turn * value - last, value
        return carry

    lax.fori_loop(0, SLOTS, tables, 0)

    scale_grid = 1.0 / math.sqrt(M)
    scale_zonal = 2.0 / math.sqrt(NLON)

    arrived(out_q)
    wide = jnp.concatenate([flat_rows(grid_q[s]) for s in range(SLOTS)], axis=0)

    def grid_quarter(i, carry):
        at = pl.ds(pl.multiple_of(i * 512, 512), 512)
        values = dot(tt[at, :], wide) * scale_grid
        prod_q[at, :] = (values * pltpu.roll(values, 96, 1)).astype(BF16)
        return carry

    lax.fori_loop(0, NLON // 512, grid_quarter, 0)

    def zonal_quarter(s, carry):
        values = dot(tr[pl.ds(pl.multiple_of(s * 256, 256), 256), :], prod_q[...]) * scale_zonal
        back_q[s] = pair_rows(values.astype(BF16))
        return carry

    lax.fori_loop(0, SLOTS, zonal_quarter, 0)

    arrived(out_f)
    ret_q = exchange(back_q.at[:, pl.ds(0, DEV - 1)], lambda b, g: back_q.at[:, b * GRP + g], home_q.at[:, g0, b0], 2)

    wide = jnp.concatenate(
        [jnp.concatenate([flat_rows(grid_f[s, f]) for s in range(SLOTS)], axis=0) for f in range(FIELDS)], axis=1
    )

    def grid_full(i, carry):
        at = pl.ds(pl.multiple_of(i * 256, 256), 256)
        values = dot(tt[at, :], wide) * scale_grid
        following = jnp.concatenate([values[:, 128:], values[:, :128]], axis=1)
        prod_f[at, :] = (values * following).astype(BF16)
        return carry

    lax.fori_loop(0, NLON // 256, grid_full, 0)

    def zonal_full(s, carry):
        values = dot(tr[pl.ds(pl.multiple_of(s * 256, 256), 256), :], prod_f[...]) * scale_zonal
        for f in range(FIELDS):
            back_f[s, f] = pair_rows(values[:, f * 128 : f * 128 + 128].astype(BF16))
        return carry

    returns = []
    for i, (lo, hi) in enumerate(GROUPS):
        lax.fori_loop(lo, hi, zonal_full, 0)
        span = pl.ds(lo, hi - lo)
        returns.append(
            exchange(
                back_f.at[span, :, pl.ds(0, DEV - 1)],
                lambda b, g, span=span: back_f.at[span, :, b * GRP + g],
                home_f.at[span, g0, :, b0],
                3 + i,
            )
        )

    r = iota((2 * ROWS, 2 * ROWS), 0)
    j = iota((2 * ROWS, 2 * ROWS), 1)
    hit = (j & 127) == ((r & 63) << 1) + ((r >> 6) & 1)
    both_signs = jnp.where(hit, jnp.where((r >= ROWS) & (j >= ROWS), -1.0, 1.0), 0.0).astype(BF16)
    scale_out = 1.0 / math.sqrt(NLAT)

    def direct(s):
        halves = []
        for h in range(2):
            parts = [flat_rows(home_f[s, h * 4 + blk]) for blk in range(4)]
            quarters = [flat_rows(home_q[s, h * 4 + q]).astype(F32) for q in range(4)]
            mixed = []
            for f in range(FIELDS):
                moved = [pltpu.roll(quarters[q], (32 * (q - f)) % 128, 1) if q != f else quarters[q] for q in range(4)]
                mixed.append(
                    jnp.where(
                        lane_group < 2,
                        jnp.where(lane_group == 0, moved[0], moved[1]),
                        jnp.where(lane_group == 2, moved[2], moved[3]),
                    )
                )
            parts.append(jnp.concatenate(mixed, axis=0).astype(BF16))
            halves.append(jnp.concatenate(parts, axis=1))
        folded = dot(both_signs, jnp.concatenate(halves, axis=0)).astype(BF16)
        result = lax.dot_general(folded, leg_v[s], NT, preferred_element_type=F32)
        chosen = jnp.where(((degree - waves[s]) & 1) == 0, result[:ROWS], result[ROWS:])
        out_v[s] = jnp.where(degree >= waves[s], chosen * scale_out, 0.0)

    arrived(ret_q)
    puts = []
    for i, (lo, hi) in enumerate(GROUPS):
        arrived(returns[i])
        for s in range(lo, hi):
            direct(s)
            puts.append(pltpu.make_async_copy(out_v.at[s], out_hbm.at[s], out_sem.at[s]))
            puts[-1].start()
    for handle in [out_q, out_f, ret_q] + returns:
        handle[1].wait_send()
    for put in puts:
        put.wait()


def on_device(spectral, legendre, owner_table):
    anywhere = pl.BlockSpec(memory_space=pl.ANY)
    out = pl.pallas_call(
        kernel,
        out_shape=jax.ShapeDtypeStruct((SLOTS, ROWS, N), F32),
        in_specs=[
            pl.BlockSpec(memory_space=pltpu.SMEM),
            pl.BlockSpec(memory_space=pltpu.VMEM),
            anywhere,
            anywhere,
        ],
        out_specs=anywhere,
        scratch_shapes=[
            pltpu.VMEM((SLOTS, ROWS, N), BF16),
            pltpu.VMEM((SLOTS, N, N), BF16),
            pltpu.VMEM((SLOTS, 2 * ROWS, N), BF16),
            pltpu.VMEM((SLOTS, GRP, LEV, 2, 128), BF16),
            pltpu.VMEM((SLOTS, GRP, FIELDS, LEV, 2, 128), BF16),
            pltpu.VMEM((SLOTS, DEV, 2, 128), BF16),
            pltpu.VMEM((SLOTS, FIELDS, DEV, 2, 128), BF16),
            pltpu.VMEM((NLON, 2 * M), BF16),
            pltpu.VMEM((2 * M, NLON), BF16),
            pltpu.VMEM((NLON, 128), BF16),
            pltpu.VMEM((NLON, 512), BF16),
            pltpu.VMEM((SLOTS, DEV, 2, 128), BF16),
            pltpu.VMEM((SLOTS, FIELDS, DEV, 2, 128), BF16),
            pltpu.VMEM((SLOTS, GRP, LEV, 2, 128), BF16),
            pltpu.VMEM((SLOTS, GRP, FIELDS, LEV, 2, 128), BF16),
            pltpu.VMEM((SLOTS, ROWS, N), F32),
            pltpu.SemaphoreType.DMA((3,)),
            pltpu.SemaphoreType.DMA((SLOTS,)),
            pltpu.SemaphoreType.DMA((3 + len(GROUPS),)),
            pltpu.SemaphoreType.DMA((3 + len(GROUPS),)),
            pltpu.SemaphoreType.DMA((3 + len(GROUPS),)),
            pltpu.SemaphoreType.REGULAR,
        ],
        compiler_params=pltpu.CompilerParams(
            collective_id=0, has_side_effects=True, vmem_limit_bytes=60 << 20
        ),
    )(
        owner_table,
        owner_table.reshape(1, M),
        spectral.reshape(SLOTS, ROWS, N),
        legendre,
    )
    return out.reshape(SLOTS, 2, FIELDS, LEV, N)


def solution(mesh):
    placed = (P(("band", "grp"), None, None, None, None), P(("band", "grp"), None, None), P())
    return jax.shard_map(
        on_device,
        mesh=mesh,
        in_specs=placed,
        out_specs=P(("band", "grp"), None, None, None, None),
        check_vma=False,
    )
```

```python
import functools
import math

import jax
import jax.numpy as jnp
from jax import lax
from jax.experimental import pallas as pl
from jax.experimental.pallas import tpu as pltpu
from jax.sharding import PartitionSpec as P

M = 640
N = 640
NLAT = 1280
NLON = 2560
FIELDS = 4
LEV = 16
SLOTS = 5
BAND = 16
GRP = 8
DEV = BAND * GRP
ROWS = 2 * FIELDS * LEV
MESH = pl.DeviceIdType.MESH
F32 = jnp.float32
BF16 = jnp.bfloat16
RETURNS = ((0, 2), (2, 4), (4, 5))
HALF = NLON // 2
PART = 3 * 2 * DEV
NT = (((1,), (1,)), ((), ()))


def dot(a, b):
    return jnp.dot(a, b, preferred_element_type=F32)


def iota(shape, axis):
    return lax.broadcasted_iota(jnp.int32, shape, axis)


def turned_cos(turns, quarter):
    whole = jnp.floor(turns * (4.0 / NLON) + 0.5)
    x = (turns - whole * (NLON / 4.0)) * (2.0 * math.pi / NLON)
    y = x * x
    cosine = 1.0 + y * (-0.5 + y * (1.0 / 24 + y * (-1.0 / 720 + y * (1.0 / 40320))))
    sine = x * (1.0 + y * (-1.0 / 6 + y * (1.0 / 120 + y * (-1.0 / 5040 + y * (1.0 / 362880)))))
    k = whole + quarter
    k = k - 4.0 * jnp.floor(k * 0.25)
    odd = (k == 1.0) | (k == 3.0)
    value = jnp.where(odd, sine, cosine)
    return jnp.where((k == 1.0) | (k == 2.0), -value, value)


def pair_rows(x):
    return x.reshape(x.shape[0] // 2, 2, 128)


def flat_rows(x):
    return x.reshape(-1, 128)


def swap_halves(first, second, low):
    a, b = pltpu.roll(first, 64, 1), pltpu.roll(second, 64, 1)
    return jnp.where(low, a, b), jnp.where(low, b, a)


def pick_group(lane_group, x):
    return jnp.where(
        lane_group < 2,
        jnp.where(lane_group == 0, x[0], x[1]),
        jnp.where(lane_group == 2, x[2], x[3]),
    )


def kernel(
    tab_smem, tab_ref, spec_hbm, leg_hbm, out_v,
    spec_v, leg_v, x_v, send_a, send_b, grid_a, grid_b, tt, tr, tr4, prod_a, prod_b,
    back_a, back_b, home_a, home_b,
    in_sem, own_sem, ssem, rsem, plane_sem,
):
    b0 = lax.axis_index("band")
    g0 = lax.axis_index("grp")
    me = b0 * GRP + g0

    barrier = pltpu.get_barrier_semaphore()
    for i in range(1, BAND):
        pl.semaphore_signal(barrier, inc=1, device_id=((b0 + i) & (BAND - 1), g0), device_id_type=MESH)
    for i in range(1, GRP):
        pl.semaphore_signal(barrier, inc=1, device_id=(b0, (g0 + i) & (GRP - 1)), device_id_type=MESH)

    cols_a, cols_b = pl.ds(0, 256), pl.ds(256, 384)
    get_spec = pltpu.make_async_copy(spec_hbm, spec_v, in_sem.at[0])
    get_a = pltpu.make_async_copy(leg_hbm.at[:, :, cols_a], leg_v.at[:, :, cols_a], in_sem.at[1])
    get_b = pltpu.make_async_copy(leg_hbm.at[:, :, cols_b], leg_v.at[:, :, cols_b], in_sem.at[2])
    get_spec.start()
    get_a.start()
    get_b.start()

    degree = iota((1, N), 1)
    waves = [tab_smem[me * SLOTS + s] for s in range(SLOTS)]
    ordered = [(waves[2 * p] & 1) == 0 for p in range(2)]

    def sorted_pairs(x):
        pairs = []
        for p in range(2):
            pairs.append(jnp.where(ordered[p], x[2 * p], x[2 * p + 1]))
            pairs.append(jnp.where(ordered[p], x[2 * p + 1], x[2 * p]))
        return pairs + [x[4]]

    r = iota((ROWS, ROWS), 0)
    perm = jnp.where(iota((ROWS, ROWS), 1) == (r & 1) * 64 + (r >> 1), 1.0, 0.0).astype(BF16)
    get_spec.wait()
    for s in range(SLOTS):
        rows = dot(perm, spec_v[s])
        rows = jnp.where(degree >= waves[s], rows, 0.0)
        flip = jnp.where(((degree - waves[s]) & 1) == 1, -1.0, 1.0)
        x_v[s, :ROWS] = rows.astype(BF16)
        x_v[s, ROWS:] = (rows * flip).astype(BF16)

    pl.semaphore_wait(barrier, BAND - 1 + GRP - 1)
    for i in range(1, GRP):
        pl.semaphore_signal(plane_sem, inc=1, device_id=(b0, (g0 + i) & (GRP - 1)), device_id_type=MESH)

    scale_in = 1.0 / math.sqrt(N)
    lane = iota((32, 128), 1)
    low = lane < 64
    lane_group = lane >> 5

    def inverse(first, width):
        parts = [(dot(x_v[s], leg_v[s, :, first : first + width]) * scale_in).astype(BF16) for s in range(SLOTS)]
        return sorted_pairs(parts)

    def by_halves(part, h, base, put):
        for blk in range(2):
            at = base + blk * 128
            x = [part[h * 128 + 32 * f : h * 128 + 32 * f + 32, at : at + 128].astype(F32) for f in range(FIELDS)]
            y = [pltpu.roll(v, 64, 1) for v in x]
            for j in range(2):
                put(h * 4 + 2 * blk, j, jnp.where(low, x[2 * j], y[2 * j + 1]))
                put(h * 4 + 2 * blk + 1, j, jnp.where(low, y[2 * j], x[2 * j + 1]))

    x0, y0, z0, c0 = b0 >> 2, b0 & 3, g0 >> 1, g0 & 1

    def peer(t):
        turn = t >> 1
        dx = turn & 3
        dy = ((turn >> 2) + turn) & 3
        dz = ((turn >> 4) + turn) & 3
        b = (((x0 + dx) & 3) << 2) + ((y0 + dy) & 3)
        g = (((z0 + dz) & 3) << 1) + ((c0 + t) & 1)
        return b, g

    def exchange(piece, source, target, which):
        def step(t, carry):
            b, g = peer(t)
            pltpu.make_async_remote_copy(
                src_ref=source(b, g), dst_ref=target, send_sem=ssem.at[which], recv_sem=rsem.at[which],
                device_id=(b, g), device_id_type=MESH,
            ).start()
            return carry

        lax.fori_loop(1, DEV, step, 0)
        own = pltpu.make_async_copy(source(b0, g0), target, own_sem.at[which])
        own.start()
        every = pltpu.make_async_remote_copy(
            src_ref=piece, dst_ref=piece, send_sem=ssem.at[which], recv_sem=rsem.at[which],
            device_id=(b0, g0), device_id_type=MESH,
        )
        return own, every

    def arrived(handle):
        handle[0].wait()
        handle[1].wait_recv()

    others = pl.ds(0, DEV - 1)
    get_a.wait()
    for s, part in enumerate(inverse(0, 256)):

        def put_a(g, j, value, s=s):
            send_a[g, 2 * s + j] = pair_rows(value.astype(BF16))

        for h in range(2):
            by_halves(part, h, 0, put_a)

    pl.semaphore_wait(plane_sem, GRP - 1)
    out_a = exchange(grid_a.at[:, others], lambda b, g: send_a.at[g, :, b], grid_a.at[:, me], 0)

    get_b.wait()
    for s, part in enumerate(inverse(256, 384)):

        def put_b(g, j, value, s=s):
            send_b[g, 3 * s + j] = pair_rows(value.astype(BF16))

        for h in range(2):
            by_halves(part, h, 0, put_b)
            x = [part[h * 128 + 32 * f : h * 128 + 32 * f + 32, 256:384].astype(F32) for f in range(FIELDS)]
            turned = [[v if i == 0 else pltpu.roll(v, 32 * i, 1) for i in range(4)] for v in x]
            for q in range(4):
                put_b(h * 4 + q, 2, pick_group(lane_group, [turned[f][(f - q) % 4] for f in range(FIELDS)]))

    out_b = exchange(grid_b.at[:, others], lambda b, g: send_b.at[g, :, b], grid_b.at[:, me], 1)

    tab = tab_ref[...].reshape(1, M).astype(F32)
    high = jnp.floor(tab * (1.0 / 32))
    rest = tab - 32.0 * high
    row8 = iota((8, M), 0)
    split_rows = jnp.where(row8 == 0, high, jnp.where(row8 == 1, rest, 0.0)).astype(BF16)
    high_rows = jnp.broadcast_to(high, (128, M)).astype(BF16)
    rest_rows = jnp.broadcast_to(rest, (128, M)).astype(BF16)

    def wave_row(s):
        pick = jnp.where(iota((M, 256), 0) == (iota((M, 256), 1) >> 1) * SLOTS + s, 1.0, 0.0).astype(BF16)
        found = dot(split_rows, pick)
        return found[0:1] * 32.0 + found[1:2]

    def wave_column(s):
        pick = jnp.where(iota((256, M), 1) == (iota((256, M), 0) >> 1) * SLOTS + s, 1.0, 0.0).astype(BF16)
        found = 32.0 * lax.dot_general(pick, high_rows, NT, preferred_element_type=F32)
        return found + lax.dot_general(pick, rest_rows, NT, preferred_element_type=F32)

    def is_even(wave):
        return wave - 2.0 * jnp.floor(wave * 0.5) == 0.0

    def split_pair(first, second):
        even = is_even(first)
        return jnp.where(even, first, second), jnp.where(even, second, first)

    def fill_tt(wave, at, odd_at=None):
        quarter = (iota((1, 256), 1) & 1).astype(F32)
        turn = 2.0 * turned_cos(wave * 128.0, 0.0)
        if odd_at is not None:
            even = is_even(wave)

        def strip(i, carry):
            line = (iota((32, 256), 0) + i * 32).astype(F32)
            last = turned_cos(wave * line, quarter)
            value = turned_cos(wave * (line + 128.0), quarter)
            for a in range(HALF // 128):
                rows = pl.ds(pl.multiple_of(a * 128 + i * 32, 32), 32)
                if odd_at is None:
                    tt[rows, at : at + 256] = last.astype(BF16)
                else:
                    tt[rows, at : at + 256] = jnp.where(even, last, 0.0).astype(BF16)
                    tt[rows, odd_at : odd_at + 256] = jnp.where(even, 0.0, last).astype(BF16)
                value, last = turn * value - last, value
            return carry

        lax.fori_loop(0, 4, strip, 0)

    def fill_tr(wave, at):
        for i in range(4):
            w = wave[i * 64 : i * 64 + 64]
            line = iota((64, 128), 1).astype(F32)
            quarter = (iota((64, 128), 0) & 1).astype(F32)
            turn = 2.0 * turned_cos(w * 128.0, 0.0)
            last = turned_cos(w * line, quarter)
            value = turned_cos(w * (line + 128.0), quarter)
            even = is_even(w)
            for a in range(HALF // 128):
                cols = slice(a * 128, a * 128 + 128)
                if at is not None:
                    tr[at + i * 64 : at + i * 64 + 64, cols] = last.astype(BF16)
                else:
                    tr4[i * 64 : i * 64 + 64, cols] = jnp.where(even, last, 0.0).astype(BF16)
                    cols = slice(HALF + a * 128, HALF + a * 128 + 128)
                    tr4[i * 64 : i * 64 + 64, cols] = jnp.where(even, 0.0, last).astype(BF16)
                value, last = turn * value - last, value

    def tables():
        for p in range(2):
            even, odd = split_pair(wave_row(2 * p), wave_row(2 * p + 1))
            fill_tt(even, 256 * p)
            fill_tt(odd, PART + 256 * p)
            even, odd = split_pair(wave_column(2 * p), wave_column(2 * p + 1))
            fill_tr(even, 512 * p)
            fill_tr(odd, 512 * p + 256)
        fill_tt(wave_row(4), 512, PART + 512)
        fill_tr(wave_column(4), None)

    tables()

    scale_zonal = 2.0 / math.sqrt(NLON) / M * 2.0

    def to_grid(grid, prod, blocks):
        def waves_of(parity):
            return jnp.concatenate(
                [
                    jnp.concatenate([flat_rows(grid[s * blocks + j]) for s in (parity, 2 + parity, 4)], axis=0)
                    for j in range(blocks)
                ],
                axis=1,
            )

        even_in, odd_in = waves_of(0), waves_of(1)
        step = 256
        low_lanes = iota((step, 128), 1) < 64

        def chunk(i, carry):
            start = pl.multiple_of(i * step, step)
            even = dot(tt[pl.ds(start, step), :PART], even_in)
            odd = dot(tt[pl.ds(start, step), PART:], odd_in)
            e = [even[:, j * 128 : j * 128 + 128] for j in range(blocks)]
            o = [odd[:, j * 128 : j * 128 + 128] for j in range(blocks)]
            e_next = list(swap_halves(e[0], e[1], low_lanes))
            o_next = list(swap_halves(o[0], o[1], low_lanes))
            if blocks == 3:
                e_next.append(pltpu.roll(e[2], 96, 1))
                o_next.append(pltpu.roll(o[2], 96, 1))
            for j in range(blocks):
                cols = slice(j * 128, j * 128 + 128)
                prod[pl.ds(start, step), cols] = (e[j] * e_next[j] + o[j] * o_next[j]).astype(BF16)
                prod[pl.ds(HALF + start, step), cols] = (e[j] * o_next[j] + o[j] * e_next[j]).astype(BF16)
            return carry

        lax.fori_loop(0, HALF // step, chunk, 0)

    def to_zonal(prod, back, blocks, slots):
        for s in slots:
            if s == 4:
                values = dot(tr4[...], prod[...])
            else:
                half = (s & 1) * HALF
                values = dot(tr[s * 256 : s * 256 + 256, :], prod[half : half + HALF, :])
            values = (values * scale_zonal).astype(BF16)
            for j in range(blocks):
                back[s * blocks + j] = pair_rows(values[:, j * 128 : j * 128 + 128])

    arrived(out_a)
    to_grid(grid_a, prod_a, 2)
    to_zonal(prod_a, back_a, 2, range(SLOTS))
    ret_a = exchange(back_a.at[:, others], lambda b, g: back_a.at[:, b * GRP + g], home_a.at[g0, :, b0], 2)

    arrived(out_b)
    to_grid(grid_b, prod_b, 3)
    returns = []
    for i, (first, end) in enumerate(RETURNS):
        to_zonal(prod_b, back_b, 3, range(first, end))
        span = pl.ds(3 * first, 3 * (end - first))
        returns.append(
            exchange(
                back_b.at[span, others],
                lambda b, g, span=span: back_b.at[span, b * GRP + g],
                home_b.at[g0, span, b0],
                3 + i,
            )
        )

    r = iota((2 * ROWS, 2 * ROWS), 0)
    j = iota((2 * ROWS, 2 * ROWS), 1)
    hit = (j & 127) == ((r & 63) << 1) + ((r >> 6) & 1)
    both_signs = jnp.where(hit, jnp.where((r >= ROWS) & (j >= ROWS), -1.0, 1.0), 0.0).astype(BF16)
    scale_out = 1.0 / math.sqrt(NLAT)

    def from_halves(home, h, row):
        blocks = []
        for blk in range(2):
            z = [[flat_rows(home[h * 4 + 2 * blk + i, row + j]).astype(F32) for j in range(2)] for i in range(2)]
            y = [[pltpu.roll(v, 64, 1) for v in w] for w in z]
            fields = []
            for j in range(2):
                fields.append(jnp.where(low, z[0][j], y[1][j]))
                fields.append(jnp.where(low, y[0][j], z[1][j]))
            blocks.append(jnp.concatenate(fields, axis=0).astype(BF16))
        return blocks

    def gather(s):
        halves = []
        for h in range(2):
            parts = from_halves(home_a, h, 2 * s) + from_halves(home_b, h, 3 * s)
            z = [flat_rows(home_b[h * 4 + q, 3 * s + 2]).astype(F32) for q in range(4)]
            turned = [[v if i == 0 else pltpu.roll(v, 32 * i, 1) for i in range(4)] for v in z]
            mixed = [pick_group(lane_group, [turned[q][(q - f) % 4] for q in range(4)]) for f in range(FIELDS)]
            parts.append(jnp.concatenate(mixed, axis=0).astype(BF16))
            halves.append(jnp.concatenate(parts, axis=1))
        return jnp.concatenate(halves, axis=0)

    def direct(s, rows):
        folded = dot(both_signs, rows).astype(BF16)
        result = lax.dot_general(folded, leg_v[s], NT, preferred_element_type=F32)
        chosen = jnp.where(((degree - waves[s]) & 1) == 0, result[:ROWS], result[ROWS:])
        out_v[s] = jnp.where(degree >= waves[s], chosen * scale_out, 0.0)

    arrived(ret_a)
    for i, (first, end) in enumerate(RETURNS):
        arrived(returns[i])
        rows = [gather(s) for s in range(first, end)]
        if end - first == 2:
            keep = ordered[first // 2]
            rows = [jnp.where(keep, rows[0], rows[1]), jnp.where(keep, rows[1], rows[0])]
        for s in range(first, end):
            direct(s, rows[s - first])
    for handle in [out_a, out_b, ret_a] + returns:
        handle[1].wait_send()


def on_device(spectral, legendre, owner_table):
    anywhere = pl.BlockSpec(memory_space=pl.ANY)
    moves = 3 + len(RETURNS)
    out = pl.pallas_call(
        kernel,
        out_shape=pltpu.VMEM((SLOTS, ROWS, N), F32),
        in_specs=[
            pl.BlockSpec(memory_space=pltpu.SMEM),
            pl.BlockSpec(memory_space=pltpu.VMEM),
            anywhere,
            anywhere,
        ],
        out_specs=pl.BlockSpec(memory_space=pltpu.VMEM),
        scratch_shapes=[
            pltpu.VMEM((SLOTS, ROWS, N), BF16),
            pltpu.VMEM((SLOTS, N, N), BF16),
            pltpu.VMEM((SLOTS, 2 * ROWS, N), BF16),
            pltpu.VMEM((GRP, 2 * SLOTS, LEV, 2, 128), BF16),
            pltpu.VMEM((GRP, 3 * SLOTS, LEV, 2, 128), BF16),
            pltpu.VMEM((2 * SLOTS, DEV, 2, 128), BF16),
            pltpu.VMEM((3 * SLOTS, DEV, 2, 128), BF16),
            pltpu.VMEM((HALF, 2 * PART), BF16),
            pltpu.VMEM((8 * DEV, HALF), BF16),
            pltpu.VMEM((2 * DEV, NLON), BF16),
            pltpu.VMEM((NLON, 256), BF16),
            pltpu.VMEM((NLON, 384), BF16),
            pltpu.VMEM((2 * SLOTS, DEV, 2, 128), BF16),
            pltpu.VMEM((3 * SLOTS, DEV, 2, 128), BF16),
            pltpu.VMEM((GRP, 2 * SLOTS, LEV, 2, 128), BF16),
            pltpu.VMEM((GRP, 3 * SLOTS, LEV, 2, 128), BF16),
            pltpu.SemaphoreType.DMA((3,)),
            pltpu.SemaphoreType.DMA((moves,)),
            pltpu.SemaphoreType.DMA((moves,)),
            pltpu.SemaphoreType.DMA((moves,)),
            pltpu.SemaphoreType.REGULAR,
        ],
        compiler_params=pltpu.CompilerParams(
            collective_id=0, has_side_effects=True, vmem_limit_bytes=61 << 20
        ),
    )(
        owner_table,
        owner_table,
        spectral.reshape(SLOTS, ROWS, N),
        legendre,
    )
    return out.reshape(SLOTS, 2, FIELDS, LEV, N)


def solution(mesh):
    placed = (P(("band", "grp"), None, None, None, None), P(("band", "grp"), None, None), P())
    return jax.shard_map(
        on_device,
        mesh=mesh,
        in_specs=placed,
        out_specs=P(("band", "grp"), None, None, None, None),
        check_vma=False,
    )
```

```python
import functools
import math

import jax
import jax.numpy as jnp
from jax import lax
from jax.experimental import pallas as pl
from jax.experimental.pallas import tpu as pltpu
from jax.sharding import PartitionSpec as P

M = 640
N = 640
NLAT = 1280
NLON = 2560
FIELDS = 4
LEV = 16
SLOTS = 5
BAND = 16
GRP = 8
DEV = BAND * GRP
ROWS = 2 * FIELDS * LEV
MESH = pl.DeviceIdType.MESH
F32 = jnp.float32
BF16 = jnp.bfloat16
RETURNS = ((0, 2), (2, 4), (4, 5))
HALF = NLON // 2
PART = 3 * 2 * DEV
NT = (((1,), (1,)), ((), ()))


def dot(a, b):
    return jnp.dot(a, b, preferred_element_type=F32)


def iota(shape, axis):
    return lax.broadcasted_iota(jnp.int32, shape, axis)


def turned_cos(turns):
    near = turns - jnp.floor(turns * (1.0 / NLON) + 0.5) * NLON
    x = near * (math.pi / NLON)
    y = x * x
    sine = 1.0 / 6227020800
    for n in (11, 9, 7, 5, 3, 1):
        sine = (-1.0 if n % 4 == 3 else 1.0) / math.factorial(n) + y * sine
    sine = x * sine
    return 1.0 - 2.0 * (sine * sine)


def pair_rows(x):
    return x.reshape(x.shape[0] // 2, 2, 128)


def flat_rows(x):
    return x.reshape(-1, 128)


def swap_halves(first, second, low):
    a, b = pltpu.roll(first, 64, 1), pltpu.roll(second, 64, 1)
    return jnp.where(low, a, b), jnp.where(low, b, a)


def pick_group(lane_group, x):
    return jnp.where(
        lane_group < 2,
        jnp.where(lane_group == 0, x[0], x[1]),
        jnp.where(lane_group == 2, x[2], x[3]),
    )


def kernel(
    tab_smem, tab_ref, spec_hbm, leg_hbm, out_v,
    spec_v, leg_v, x_v, send_a, send_q, send_b, grid_a, grid_q, grid_b, tt, tr, tr4, prod_a, prod_q, prod_b,
    back_a, back_q, back_b, home_a, home_q, home_b,
    in_sem, own_sem, ssem, rsem, plane_sem,
):
    b0 = lax.axis_index("band")
    g0 = lax.axis_index("grp")
    me = b0 * GRP + g0

    parts = [(0, 256), (256, 128), (384, 256)]
    get_spec = pltpu.make_async_copy(spec_hbm, spec_v, in_sem.at[0])
    get_spec.start()
    get_leg = []
    for i, (first, width) in enumerate(parts):
        cols = pl.ds(first, width)
        get_leg.append(pltpu.make_async_copy(leg_hbm.at[:, :, cols], leg_v.at[:, :, cols], in_sem.at[1 + i]))
        get_leg[-1].start()

    barrier = pltpu.get_barrier_semaphore()
    for i in range(1, BAND):
        pl.semaphore_signal(barrier, inc=1, device_id=((b0 + i) & (BAND - 1), g0), device_id_type=MESH)
    for i in range(1, GRP):
        pl.semaphore_signal(barrier, inc=1, device_id=(b0, (g0 + i) & (GRP - 1)), device_id_type=MESH)

    degree = iota((1, N), 1)
    waves = [tab_smem[me * SLOTS + s] for s in range(SLOTS)]
    ordered = [(waves[2 * p] & 1) == 0 for p in range(2)]

    def sorted_pairs(x):
        pairs = []
        for p in range(2):
            pairs.append(jnp.where(ordered[p], x[2 * p], x[2 * p + 1]))
            pairs.append(jnp.where(ordered[p], x[2 * p + 1], x[2 * p]))
        return pairs + [x[4]]

    r = iota((ROWS, ROWS), 0)
    perm = jnp.where(iota((ROWS, ROWS), 1) == (r & 1) * 64 + (r >> 1), 1.0, 0.0).astype(BF16)
    get_spec.wait()
    for s in range(SLOTS):
        rows = dot(perm, spec_v[s])
        rows = jnp.where(degree >= waves[s], rows, 0.0)
        flip = jnp.where(((degree - waves[s]) & 1) == 1, -1.0, 1.0)
        x_v[s, :ROWS] = rows.astype(BF16)
        x_v[s, ROWS:] = (rows * flip).astype(BF16)

    pl.semaphore_wait(barrier, BAND - 1 + GRP - 1)
    for i in range(1, GRP):
        pl.semaphore_signal(plane_sem, inc=1, device_id=(b0, (g0 + i) & (GRP - 1)), device_id_type=MESH)

    scale_in = 1.0 / math.sqrt(N)
    lane = iota((32, 128), 1)
    low = lane < 64
    lane_group = lane >> 5

    def inverse(first, width):
        parts = [(dot(x_v[s], leg_v[s, :, first : first + width]) * scale_in).astype(BF16) for s in range(SLOTS)]
        return sorted_pairs(parts)

    def by_halves(part, h, put):
        for blk in range(2):
            at = blk * 128
            x = [part[h * 128 + 32 * f : h * 128 + 32 * f + 32, at : at + 128].astype(F32) for f in range(FIELDS)]
            y = [pltpu.roll(v, 64, 1) for v in x]
            for j in range(2):
                put(h * 4 + 2 * blk, j, jnp.where(low, x[2 * j], y[2 * j + 1]))
                put(h * 4 + 2 * blk + 1, j, jnp.where(low, y[2 * j], x[2 * j + 1]))

    x0, y0, z0, c0 = b0 >> 2, b0 & 3, g0 >> 1, g0 & 1

    def exchange(piece, source, target, which):
        def step(i, carry, first=0):
            for t in range(first, 8):
                j = t >> 1
                b = (((x0 + j) & 3) << 2) + ((y0 + i + j) & 3)
                g = (((z0 + (i >> 2) + j) & 3) << 1) + (c0 ^ (t & 1))
                pltpu.make_async_remote_copy(
                    src_ref=source(b, g), dst_ref=target, send_sem=ssem.at[which], recv_sem=rsem.at[which],
                    device_id=(b, g), device_id_type=MESH,
                ).start()
            return carry

        step(0, 0, 1)
        lax.fori_loop(1, DEV // 8, step, 0)
        own = pltpu.make_async_copy(source(b0, g0), target, own_sem.at[which])
        own.start()
        every = pltpu.make_async_remote_copy(
            src_ref=piece, dst_ref=piece, send_sem=ssem.at[which], recv_sem=rsem.at[which],
            device_id=(b0, g0), device_id_type=MESH,
        )
        return own, every

    def arrived(handle):
        handle[0].wait()
        handle[1].wait_recv()

    others = pl.ds(0, DEV - 1)

    def halves_out(which, send):
        get_leg[which].wait()
        for s, part in enumerate(inverse(*parts[which])):

            def put(g, j, value, s=s):
                send[g, 2 * s + j] = pair_rows(value.astype(BF16))

            for h in range(2):
                by_halves(part, h, put)

    halves_out(0, send_a)
    pl.semaphore_wait(plane_sem, GRP - 1)
    out_a = exchange(grid_a.at[:, others], lambda b, g: send_a.at[g, :, b], grid_a.at[:, me], 0)

    get_leg[1].wait()
    for s, part in enumerate(inverse(*parts[1])):
        for h in range(2):
            x = [part[h * 128 + 32 * f : h * 128 + 32 * f + 32].astype(F32) for f in range(FIELDS)]
            turned = [[v if i == 0 else pltpu.roll(v, 32 * i, 1) for i in range(4)] for v in x]
            for q in range(4):
                value = pick_group(lane_group, [turned[f][(f - q) % 4] for f in range(FIELDS)])
                send_q[h * 4 + q, s] = pair_rows(value.astype(BF16))
    out_q = exchange(grid_q.at[:, others], lambda b, g: send_q.at[g, :, b], grid_q.at[:, me], 1)

    halves_out(2, send_b)
    out_b = exchange(grid_b.at[:, others], lambda b, g: send_b.at[g, :, b], grid_b.at[:, me], 2)

    tab = tab_ref[...].reshape(1, M).astype(F32)
    high = jnp.floor(tab * (1.0 / 32))
    rest = tab - 32.0 * high
    row8 = iota((8, M), 0)
    split_rows = jnp.where(row8 == 0, high, jnp.where(row8 == 1, rest, 0.0)).astype(BF16)
    high_rows = jnp.broadcast_to(high, (128, M)).astype(BF16)
    rest_rows = jnp.broadcast_to(rest, (128, M)).astype(BF16)

    def wave_row(s):
        pick = jnp.where(iota((M, 256), 0) == (iota((M, 256), 1) >> 1) * SLOTS + s, 1.0, 0.0).astype(BF16)
        found = dot(split_rows, pick)
        return found[0:1] * 32.0 + found[1:2]

    def wave_column(s):
        pick = jnp.where(iota((256, M), 1) == (iota((256, M), 0) >> 1) * SLOTS + s, 1.0, 0.0).astype(BF16)
        found = 32.0 * lax.dot_general(pick, high_rows, NT, preferred_element_type=F32)
        return found + lax.dot_general(pick, rest_rows, NT, preferred_element_type=F32)

    def is_even(wave):
        return wave - 2.0 * jnp.floor(wave * 0.5) == 0.0

    def split_pair(first, second):
        even = is_even(first)
        return jnp.where(even, first, second), jnp.where(even, second, first)

    def fill_tt(wave, at, odd_at=None):
        quarter = ((iota((1, 256), 1) & 1) * (NLON // 4)).astype(F32)
        turn = 2.0 * turned_cos(wave * 64.0)
        if odd_at is not None:
            even = is_even(wave)

        def strip(i, carry):
            line = (iota((32, 256), 0) + i * 32).astype(F32)
            turns = wave * line + quarter
            last = turned_cos(turns)
            value = turned_cos(turns + wave * 64.0)
            for a in range(HALF // 64):
                rows = pl.ds(pl.multiple_of(a * 64 + i * 32, 32), 32)
                if odd_at is None:
                    tt[rows, at : at + 256] = last.astype(BF16)
                else:
                    tt[rows, at : at + 256] = jnp.where(even, last, 0.0).astype(BF16)
                    tt[rows, odd_at : odd_at + 256] = jnp.where(even, 0.0, last).astype(BF16)
                value, last = turn * value - last, value
            return carry

        lax.fori_loop(0, 2, strip, 0)

    def fill_tr(wave, at):
        for i in range(4):
            w = wave[i * 64 : i * 64 + 64]
            line = iota((64, 128), 1).astype(F32)
            quarter = ((iota((64, 128), 0) & 1) * (NLON // 4)).astype(F32)
            step = w * 128.0
            turn = 2.0 * turned_cos(step)
            turns = w * line + quarter
            last = turned_cos(turns)
            value = turned_cos(turns + step)
            even = is_even(w)
            for a in range(HALF // 128):
                cols = slice(a * 128, a * 128 + 128)
                if at is not None:
                    tr[at + i * 64 : at + i * 64 + 64, cols] = last.astype(BF16)
                else:
                    tr4[i * 64 : i * 64 + 64, cols] = jnp.where(even, last, 0.0).astype(BF16)
                    cols = slice(HALF + a * 128, HALF + a * 128 + 128)
                    tr4[i * 64 : i * 64 + 64, cols] = jnp.where(even, 0.0, last).astype(BF16)
                value, last = turn * value - last, value

    def tables():
        for p in range(2):
            even, odd = split_pair(wave_row(2 * p), wave_row(2 * p + 1))
            fill_tt(even, 256 * p)
            fill_tt(odd, PART + 256 * p)
            even, odd = split_pair(wave_column(2 * p), wave_column(2 * p + 1))
            fill_tr(even, 512 * p)
            fill_tr(odd, 512 * p + 256)
        fill_tt(wave_row(4), 512, PART + 512)
        fill_tr(wave_column(4), None)

    tables()

    scale_zonal = 2.0 / math.sqrt(NLON) / M * 2.0

    def to_grid(grid, prod, blocks):
        def waves_of(parity):
            return jnp.concatenate(
                [
                    jnp.concatenate([flat_rows(grid[s * blocks + j]) for s in (parity, 2 + parity, 4)], axis=0)
                    for j in range(blocks)
                ],
                axis=1,
            )

        even_in, odd_in = waves_of(0), waves_of(1)
        step = 256
        low_lanes = iota((step, 128), 1) < 64

        def chunk(i, carry):
            start = pl.multiple_of(i * step, step)
            even = dot(tt[pl.ds(start, step), :PART], even_in)
            odd = dot(tt[pl.ds(start, step), PART:], odd_in)
            e = [even[:, j * 128 : j * 128 + 128] for j in range(blocks)]
            o = [odd[:, j * 128 : j * 128 + 128] for j in range(blocks)]
            if blocks == 2:
                e_next = swap_halves(e[0], e[1], low_lanes)
                o_next = swap_halves(o[0], o[1], low_lanes)
            else:
                e_next = [pltpu.roll(e[0], 96, 1)]
                o_next = [pltpu.roll(o[0], 96, 1)]
            for j in range(blocks):
                cols = slice(j * 128, j * 128 + 128)
                prod[pl.ds(start, step), cols] = (e[j] * e_next[j] + o[j] * o_next[j]).astype(BF16)
                prod[pl.ds(HALF + start, step), cols] = (e[j] * o_next[j] + o[j] * e_next[j]).astype(BF16)
            return carry

        lax.fori_loop(0, HALF // step, chunk, 0)

    def to_zonal(prod, back, blocks, slots):
        for s in slots:
            if s == 4:
                values = dot(tr4[...], prod[...])
            else:
                half = (s & 1) * HALF
                values = dot(tr[s * 256 : s * 256 + 256, :], prod[half : half + HALF, :])
            values = (values * scale_zonal).astype(BF16)
            for j in range(blocks):
                back[s * blocks + j] = pair_rows(values[:, j * 128 : j * 128 + 128])

    arrived(out_a)
    to_grid(grid_a, prod_a, 2)
    to_zonal(prod_a, back_a, 2, range(SLOTS))
    ret_a = exchange(back_a.at[:, others], lambda b, g: back_a.at[:, b * GRP + g], home_a.at[g0, :, b0], 3)

    arrived(out_q)
    to_grid(grid_q, prod_q, 1)
    to_zonal(prod_q, back_q, 1, range(SLOTS))
    ret_q = exchange(back_q.at[:, others], lambda b, g: back_q.at[:, b * GRP + g], home_q.at[g0, :, b0], 4)

    arrived(out_b)
    to_grid(grid_b, prod_b, 2)
    returns = []
    for i, (first, end) in enumerate(RETURNS):
        to_zonal(prod_b, back_b, 2, range(first, end))
        span = pl.ds(2 * first, 2 * (end - first))
        returns.append(
            exchange(
                back_b.at[span, others],
                lambda b, g, span=span: back_b.at[span, b * GRP + g],
                home_b.at[g0, span, b0],
                5 + i,
            )
        )

    r = iota((2 * ROWS, 2 * ROWS), 0)
    j = iota((2 * ROWS, 2 * ROWS), 1)
    hit = (j & 127) == ((r & 63) << 1) + ((r >> 6) & 1)
    both_signs = jnp.where(hit, jnp.where((r >= ROWS) & (j >= ROWS), -1.0, 1.0), 0.0).astype(BF16)
    scale_out = 1.0 / math.sqrt(NLAT)

    def from_halves(home, h, row):
        blocks = []
        for blk in range(2):
            z = [[flat_rows(home[h * 4 + 2 * blk + i, row + j]).astype(F32) for j in range(2)] for i in range(2)]
            y = [[pltpu.roll(v, 64, 1) for v in w] for w in z]
            fields = []
            for j in range(2):
                fields.append(jnp.where(low, z[0][j], y[1][j]))
                fields.append(jnp.where(low, y[0][j], z[1][j]))
            blocks.append(jnp.concatenate(fields, axis=0).astype(BF16))
        return blocks

    def gather(s):
        halves = []
        for h in range(2):
            z = [flat_rows(home_q[h * 4 + q, s]).astype(F32) for q in range(4)]
            turned = [[v if i == 0 else pltpu.roll(v, 32 * i, 1) for i in range(4)] for v in z]
            mixed = [pick_group(lane_group, [turned[q][(q - f) % 4] for q in range(4)]) for f in range(FIELDS)]
            middle = [jnp.concatenate(mixed, axis=0).astype(BF16)]
            halves.append(jnp.concatenate(from_halves(home_a, h, 2 * s) + middle + from_halves(home_b, h, 2 * s), axis=1))
        return jnp.concatenate(halves, axis=0)

    def direct(s, rows):
        folded = dot(both_signs, rows).astype(BF16)
        result = lax.dot_general(folded, leg_v[s], NT, preferred_element_type=F32)
        chosen = jnp.where(((degree - waves[s]) & 1) == 0, result[:ROWS], result[ROWS:])
        out_v[s] = jnp.where(degree >= waves[s], chosen * scale_out, 0.0)

    arrived(ret_a)
    arrived(ret_q)
    for i, (first, end) in enumerate(RETURNS):
        arrived(returns[i])
        rows = [gather(s) for s in range(first, end)]
        if end - first == 2:
            keep = ordered[first // 2]
            rows = [jnp.where(keep, rows[0], rows[1]), jnp.where(keep, rows[1], rows[0])]
        for s in range(first, end):
            direct(s, rows[s - first])
    for handle in [out_a, out_q, out_b, ret_a, ret_q] + returns:
        handle[1].wait_send()


def on_device(spectral, legendre, owner_table):
    anywhere = pl.BlockSpec(memory_space=pl.ANY)
    moves = 5 + len(RETURNS)
    out = pl.pallas_call(
        kernel,
        out_shape=pltpu.VMEM((SLOTS, ROWS, N), F32),
        in_specs=[
            pl.BlockSpec(memory_space=pltpu.SMEM),
            pl.BlockSpec(memory_space=pltpu.VMEM),
            anywhere,
            anywhere,
        ],
        out_specs=pl.BlockSpec(memory_space=pltpu.VMEM),
        scratch_shapes=[
            pltpu.VMEM((SLOTS, ROWS, N), BF16),
            pltpu.VMEM((SLOTS, N, N), BF16),
            pltpu.VMEM((SLOTS, 2 * ROWS, N), BF16),
            *[pltpu.VMEM((GRP, n * SLOTS, LEV, 2, 128), BF16) for n in (2, 1, 2)],
            *[pltpu.VMEM((n * SLOTS, DEV, 2, 128), BF16) for n in (2, 1, 2)],
            pltpu.VMEM((HALF, 2 * PART), BF16),
            pltpu.VMEM((8 * DEV, HALF), BF16),
            pltpu.VMEM((2 * DEV, NLON), BF16),
            *[pltpu.VMEM((NLON, n * 128), BF16) for n in (2, 1, 2)],
            *[pltpu.VMEM((n * SLOTS, DEV, 2, 128), BF16) for n in (2, 1, 2)],
            *[pltpu.VMEM((GRP, n * SLOTS, LEV, 2, 128), BF16) for n in (2, 1, 2)],
            pltpu.SemaphoreType.DMA((4,)),
            pltpu.SemaphoreType.DMA((moves,)),
            pltpu.SemaphoreType.DMA((moves,)),
            pltpu.SemaphoreType.DMA((moves,)),
            pltpu.SemaphoreType.REGULAR,
        ],
        compiler_params=pltpu.CompilerParams(
            collective_id=0, has_side_effects=True, vmem_limit_bytes=61 << 20
        ),
    )(
        owner_table,
        owner_table,
        spectral.reshape(SLOTS, ROWS, N),
        legendre,
    )
    return out.reshape(SLOTS, 2, FIELDS, LEV, N)


def solution(mesh):
    placed = (P(("band", "grp"), None, None, None, None), P(("band", "grp"), None, None), P())
    return jax.shard_map(
        on_device,
        mesh=mesh,
        in_specs=placed,
        out_specs=P(("band", "grp"), None, None, None, None),
        check_vma=False,
    )
```

```python
import functools
import math

import jax
import jax.numpy as jnp
from jax import lax
from jax.experimental import pallas as pl
from jax.experimental.pallas import tpu as pltpu
from jax.sharding import PartitionSpec as P

M = 640
N = 640
NLAT = 1280
NLON = 2560
FIELDS = 4
LEV = 16
SLOTS = 5
BAND = 16
GRP = 8
DEV = BAND * GRP
ROWS = 2 * FIELDS * LEV
MESH = pl.DeviceIdType.MESH
F32 = jnp.float32
BF16 = jnp.bfloat16
RETURNS = ((0, 2), (2, 4), (4, 5))
HALF = NLON // 2
PART = 3 * 2 * DEV
NT = (((1,), (1,)), ((), ()))


def dot(a, b):
    return jnp.dot(a, b, preferred_element_type=F32)


def iota(shape, axis):
    return lax.broadcasted_iota(jnp.int32, shape, axis)


def turned_cos(turns):
    near = turns - jnp.floor(turns * (1.0 / NLON) + 0.5) * NLON
    x = near * (math.pi / NLON)
    y = x * x
    sine = 1.0 / 6227020800
    for n in (11, 9, 7, 5, 3, 1):
        sine = (-1.0 if n % 4 == 3 else 1.0) / math.factorial(n) + y * sine
    sine = x * sine
    return 1.0 - 2.0 * (sine * sine)


def pair_rows(x):
    return x.reshape(x.shape[0] // 2, 2, 128)


def flat_rows(x):
    return x.reshape(-1, 128)


def swap_halves(first, second, low):
    a, b = pltpu.roll(first, 64, 1), pltpu.roll(second, 64, 1)
    return jnp.where(low, a, b), jnp.where(low, b, a)


def pick_group(lane_group, x):
    return jnp.where(
        lane_group < 2,
        jnp.where(lane_group == 0, x[0], x[1]),
        jnp.where(lane_group == 2, x[2], x[3]),
    )


def kernel(
    tab_smem, tab_ref, spec_hbm, leg_hbm, out_v,
    spec_v, leg_v, x_v, send_a, send_q, send_b, grid_a, grid_q, grid_b, tt, tr, tr4, prod_a, prod_q, prod_b,
    back_a, back_q, back_b, home_a, home_q, home_b,
    in_sem, own_sem, ssem, rsem, plane_sem,
):
    b0 = lax.axis_index("band")
    g0 = lax.axis_index("grp")
    me = b0 * GRP + g0

    parts = [(0, 256), (256, 128), (384, 256)]
    get_spec = pltpu.make_async_copy(spec_hbm, spec_v, in_sem.at[0])
    get_spec.start()
    get_leg = []
    for i, (first, width) in enumerate(parts):
        cols = pl.ds(first, width)
        get_leg.append(pltpu.make_async_copy(leg_hbm.at[:, :, cols], leg_v.at[:, :, cols], in_sem.at[1 + i]))
        get_leg[-1].start()

    barrier = pltpu.get_barrier_semaphore()
    for i in range(1, BAND):
        pl.semaphore_signal(barrier, inc=1, device_id=((b0 + i) & (BAND - 1), g0), device_id_type=MESH)
    for i in range(1, GRP):
        pl.semaphore_signal(barrier, inc=1, device_id=(b0, (g0 + i) & (GRP - 1)), device_id_type=MESH)

    degree = iota((1, N), 1)
    waves = [tab_smem[me * SLOTS + s] for s in range(SLOTS)]
    ordered = [(waves[2 * p] & 1) == 0 for p in range(2)]

    def sorted_pairs(x):
        pairs = []
        for p in range(2):
            pairs.append(jnp.where(ordered[p], x[2 * p], x[2 * p + 1]))
            pairs.append(jnp.where(ordered[p], x[2 * p + 1], x[2 * p]))
        return pairs + [x[4]]

    r = iota((ROWS, ROWS), 0)
    perm = jnp.where(iota((ROWS, ROWS), 1) == (r & 1) * 64 + (r >> 1), 1.0, 0.0).astype(BF16)
    get_spec.wait()
    for s in range(SLOTS):
        rows = dot(perm, spec_v[s])
        rows = jnp.where(degree >= waves[s], rows, 0.0)
        flip = jnp.where(((degree - waves[s]) & 1) == 1, -1.0, 1.0)
        x_v[s, :ROWS] = rows.astype(BF16)
        x_v[s, ROWS:] = (rows * flip).astype(BF16)

    pl.semaphore_wait(barrier, BAND - 1 + GRP - 1)
    for i in range(1, GRP):
        pl.semaphore_signal(plane_sem, inc=1, device_id=(b0, (g0 + i) & (GRP - 1)), device_id_type=MESH)

    scale_in = 1.0 / math.sqrt(N)
    lane = iota((32, 128), 1)
    low = lane < 64
    lane_group = lane >> 5

    def inverse(first, width):
        parts = [(dot(x_v[s], leg_v[s, :, first : first + width]) * scale_in).astype(BF16) for s in range(SLOTS)]
        return sorted_pairs(parts)

    def by_halves(part, h, put):
        for blk in range(2):
            at = blk * 128
            x = [part[h * 128 + 32 * f : h * 128 + 32 * f + 32, at : at + 128].astype(F32) for f in range(FIELDS)]
            y = [pltpu.roll(v, 64, 1) for v in x]
            for j in range(2):
                put(h * 4 + 2 * blk, j, jnp.where(low, x[2 * j], y[2 * j + 1]))
                put(h * 4 + 2 * blk + 1, j, jnp.where(low, y[2 * j], x[2 * j + 1]))

    x0, y0, z0, c0 = b0 >> 2, b0 & 3, g0 >> 1, g0 & 1

    def exchange(piece, source, target, which):
        def step(i, carry, first=0):
            for t in range(first, 8):
                j = (0, 1, 3, 2)[t >> 1]
                b = (((x0 + j) & 3) << 2) + ((y0 + i + j) & 3)
                g = (((z0 + (i >> 2) + i - j) & 3) << 1) + (c0 ^ (t & 1))
                pltpu.make_async_remote_copy(
                    src_ref=source(b, g), dst_ref=target, send_sem=ssem.at[which], recv_sem=rsem.at[which],
                    device_id=(b, g), device_id_type=MESH,
                ).start()
            return carry

        step(0, 0, 1)
        lax.fori_loop(1, DEV // 8, step, 0)
        own = pltpu.make_async_copy(source(b0, g0), target, own_sem.at[which])
        own.start()
        every = pltpu.make_async_remote_copy(
            src_ref=piece, dst_ref=piece, send_sem=ssem.at[which], recv_sem=rsem.at[which],
            device_id=(b0, g0), device_id_type=MESH,
        )
        return own, every

    def arrived(handle):
        handle[0].wait()
        handle[1].wait_recv()

    others = pl.ds(0, DEV - 1)

    def halves_out(which, send):
        get_leg[which].wait()
        for s, part in enumerate(inverse(*parts[which])):

            def put(g, j, value, s=s):
                send[g, 2 * s + j] = pair_rows(value.astype(BF16))

            for h in range(2):
                by_halves(part, h, put)

    halves_out(0, send_a)
    pl.semaphore_wait(plane_sem, GRP - 1)
    out_a = exchange(grid_a.at[:, others], lambda b, g: send_a.at[g, :, b], grid_a.at[:, me], 0)

    get_leg[1].wait()
    for s, part in enumerate(inverse(*parts[1])):
        for h in range(2):
            x = [part[h * 128 + 32 * f : h * 128 + 32 * f + 32].astype(F32) for f in range(FIELDS)]
            turned = [[v if i == 0 else pltpu.roll(v, 32 * i, 1) for i in range(4)] for v in x]
            for q in range(4):
                value = pick_group(lane_group, [turned[f][(f - q) % 4] for f in range(FIELDS)])
                send_q[h * 4 + q, s] = pair_rows(value.astype(BF16))
    out_q = exchange(grid_q.at[:, others], lambda b, g: send_q.at[g, :, b], grid_q.at[:, me], 1)

    halves_out(2, send_b)
    out_b = exchange(grid_b.at[:, others], lambda b, g: send_b.at[g, :, b], grid_b.at[:, me], 2)

    tab = tab_ref[...].reshape(1, M).astype(F32)
    high = jnp.floor(tab * (1.0 / 32))
    rest = tab - 32.0 * high
    row8 = iota((8, M), 0)
    split_rows = jnp.where(row8 == 0, high, jnp.where(row8 == 1, rest, 0.0)).astype(BF16)
    high_rows = jnp.broadcast_to(high, (128, M)).astype(BF16)
    rest_rows = jnp.broadcast_to(rest, (128, M)).astype(BF16)

    def wave_row(s):
        pick = jnp.where(iota((M, 256), 0) == (iota((M, 256), 1) >> 1) * SLOTS + s, 1.0, 0.0).astype(BF16)
        found = dot(split_rows, pick)
        return found[0:1] * 32.0 + found[1:2]

    def wave_column(s):
        pick = jnp.where(iota((256, M), 1) == (iota((256, M), 0) >> 1) * SLOTS + s, 1.0, 0.0).astype(BF16)
        found = 32.0 * lax.dot_general(pick, high_rows, NT, preferred_element_type=F32)
        return found + lax.dot_general(pick, rest_rows, NT, preferred_element_type=F32)

    def is_even(wave):
        return wave - 2.0 * jnp.floor(wave * 0.5) == 0.0

    def split_pair(first, second):
        even = is_even(first)
        return jnp.where(even, first, second), jnp.where(even, second, first)

    def fill_tt(wave, at, odd_at=None):
        quarter = ((iota((1, 256), 1) & 1) * (NLON // 4)).astype(F32)
        turn = 2.0 * turned_cos(wave * 64.0)
        if odd_at is not None:
            even = is_even(wave)

        def strip(i, carry):
            line = (iota((32, 256), 0) + i * 32).astype(F32)
            turns = wave * line + quarter
            last = turned_cos(turns)
            value = turned_cos(turns + wave * 64.0)
            for a in range(HALF // 64):
                rows = pl.ds(pl.multiple_of(a * 64 + i * 32, 32), 32)
                if odd_at is None:
                    tt[rows, at : at + 256] = last.astype(BF16)
                else:
                    tt[rows, at : at + 256] = jnp.where(even, last, 0.0).astype(BF16)
                    tt[rows, odd_at : odd_at + 256] = jnp.where(even, 0.0, last).astype(BF16)
                value, last = turn * value - last, value
            return carry

        lax.fori_loop(0, 2, strip, 0)

    def fill_tr(wave, at):
        for i in range(4):
            w = wave[i * 64 : i * 64 + 64]
            line = iota((64, 128), 1).astype(F32)
            quarter = ((iota((64, 128), 0) & 1) * (NLON // 4)).astype(F32)
            step = w * 128.0
            turn = 2.0 * turned_cos(step)
            turns = w * line + quarter
            last = turned_cos(turns)
            value = turned_cos(turns + step)
            even = is_even(w)
            for a in range(HALF // 128):
                cols = slice(a * 128, a * 128 + 128)
                if at is not None:
                    tr[at + i * 64 : at + i * 64 + 64, cols] = last.astype(BF16)
                else:
                    tr4[i * 64 : i * 64 + 64, cols] = jnp.where(even, last, 0.0).astype(BF16)
                    cols = slice(HALF + a * 128, HALF + a * 128 + 128)
                    tr4[i * 64 : i * 64 + 64, cols] = jnp.where(even, 0.0, last).astype(BF16)
                value, last = turn * value - last, value

    def tables():
        for p in range(2):
            even, odd = split_pair(wave_row(2 * p), wave_row(2 * p + 1))
            fill_tt(even, 256 * p)
            fill_tt(odd, PART + 256 * p)
            even, odd = split_pair(wave_column(2 * p), wave_column(2 * p + 1))
            fill_tr(even, 512 * p)
            fill_tr(odd, 512 * p + 256)
        fill_tt(wave_row(4), 512, PART + 512)
        fill_tr(wave_column(4), None)

    tables()

    scale_zonal = 2.0 / math.sqrt(NLON) / M * 2.0

    def to_grid(grid, prod, blocks):
        def waves_of(parity):
            return jnp.concatenate(
                [
                    jnp.concatenate([flat_rows(grid[s * blocks + j]) for s in (parity, 2 + parity, 4)], axis=0)
                    for j in range(blocks)
                ],
                axis=1,
            )

        even_in, odd_in = waves_of(0), waves_of(1)
        step = 256
        low_lanes = iota((step, 128), 1) < 64

        def chunk(i, carry):
            start = pl.multiple_of(i * step, step)
            even = dot(tt[pl.ds(start, step), :PART], even_in)
            odd = dot(tt[pl.ds(start, step), PART:], odd_in)
            e = [even[:, j * 128 : j * 128 + 128] for j in range(blocks)]
            o = [odd[:, j * 128 : j * 128 + 128] for j in range(blocks)]
            if blocks == 2:
                e_next = swap_halves(e[0], e[1], low_lanes)
                o_next = swap_halves(o[0], o[1], low_lanes)
            else:
                e_next = [pltpu.roll(e[0], 96, 1)]
                o_next = [pltpu.roll(o[0], 96, 1)]
            for j in range(blocks):
                cols = slice(j * 128, j * 128 + 128)
                prod[pl.ds(start, step), cols] = (e[j] * e_next[j] + o[j] * o_next[j]).astype(BF16)
                prod[pl.ds(HALF + start, step), cols] = (e[j] * o_next[j] + o[j] * e_next[j]).astype(BF16)
            return carry

        lax.fori_loop(0, HALF // step, chunk, 0)

    def to_zonal(prod, back, blocks, slots):
        for s in slots:
            if s == 4:
                values = dot(tr4[...], prod[...])
            else:
                half = (s & 1) * HALF
                values = dot(tr[s * 256 : s * 256 + 256, :], prod[half : half + HALF, :])
            values = (values * scale_zonal).astype(BF16)
            for j in range(blocks):
                back[s * blocks + j] = pair_rows(values[:, j * 128 : j * 128 + 128])

    arrived(out_a)
    to_grid(grid_a, prod_a, 2)
    to_zonal(prod_a, back_a, 2, range(SLOTS))
    ret_a = exchange(back_a.at[:, others], lambda b, g: back_a.at[:, b * GRP + g], home_a.at[g0, :, b0], 3)

    arrived(out_q)
    to_grid(grid_q, prod_q, 1)
    to_zonal(prod_q, back_q, 1, range(SLOTS))
    ret_q = exchange(back_q.at[:, others], lambda b, g: back_q.at[:, b * GRP + g], home_q.at[g0, :, b0], 4)

    arrived(out_b)
    to_grid(grid_b, prod_b, 2)
    returns = []
    for i, (first, end) in enumerate(RETURNS):
        to_zonal(prod_b, back_b, 2, range(first, end))
        span = pl.ds(2 * first, 2 * (end - first))
        returns.append(
            exchange(
                back_b.at[span, others],
                lambda b, g, span=span: back_b.at[span, b * GRP + g],
                home_b.at[g0, span, b0],
                5 + i,
            )
        )

    r = iota((2 * ROWS, 2 * ROWS), 0)
    j = iota((2 * ROWS, 2 * ROWS), 1)
    hit = (j & 127) == ((r & 63) << 1) + ((r >> 6) & 1)
    both_signs = jnp.where(hit, jnp.where((r >= ROWS) & (j >= ROWS), -1.0, 1.0), 0.0).astype(BF16)
    scale_out = 1.0 / math.sqrt(NLAT)

    def from_halves(home, h, row):
        blocks = []
        for blk in range(2):
            z = [[flat_rows(home[h * 4 + 2 * blk + i, row + j]).astype(F32) for j in range(2)] for i in range(2)]
            y = [[pltpu.roll(v, 64, 1) for v in w] for w in z]
            fields = []
            for j in range(2):
                fields.append(jnp.where(low, z[0][j], y[1][j]))
                fields.append(jnp.where(low, y[0][j], z[1][j]))
            blocks.append(jnp.concatenate(fields, axis=0).astype(BF16))
        return blocks

    def gather(s):
        halves = []
        for h in range(2):
            z = [flat_rows(home_q[h * 4 + q, s]).astype(F32) for q in range(4)]
            turned = [[v if i == 0 else pltpu.roll(v, 32 * i, 1) for i in range(4)] for v in z]
            mixed = [pick_group(lane_group, [turned[q][(q - f) % 4] for q in range(4)]) for f in range(FIELDS)]
            middle = [jnp.concatenate(mixed, axis=0).astype(BF16)]
            halves.append(jnp.concatenate(from_halves(home_a, h, 2 * s) + middle + from_halves(home_b, h, 2 * s), axis=1))
        return jnp.concatenate(halves, axis=0)

    def direct(s, rows):
        folded = dot(both_signs, rows).astype(BF16)
        result = lax.dot_general(folded, leg_v[s], NT, preferred_element_type=F32)
        chosen = jnp.where(((degree - waves[s]) & 1) == 0, result[:ROWS], result[ROWS:])
        out_v[s] = jnp.where(degree >= waves[s], chosen * scale_out, 0.0)

    arrived(ret_a)
    arrived(ret_q)
    for i, (first, end) in enumerate(RETURNS):
        arrived(returns[i])
        rows = [gather(s) for s in range(first, end)]
        if end - first == 2:
            keep = ordered[first // 2]
            rows = [jnp.where(keep, rows[0], rows[1]), jnp.where(keep, rows[1], rows[0])]
        for s in range(first, end):
            direct(s, rows[s - first])
    for handle in [out_a, out_q, out_b, ret_a, ret_q] + returns:
        handle[1].wait_send()


def on_device(spectral, legendre, owner_table):
    anywhere = pl.BlockSpec(memory_space=pl.ANY)
    moves = 5 + len(RETURNS)
    out = pl.pallas_call(
        kernel,
        out_shape=pltpu.VMEM((SLOTS, ROWS, N), F32),
        in_specs=[
            pl.BlockSpec(memory_space=pltpu.SMEM),
            pl.BlockSpec(memory_space=pltpu.VMEM),
            anywhere,
            anywhere,
        ],
        out_specs=pl.BlockSpec(memory_space=pltpu.VMEM),
        scratch_shapes=[
            pltpu.VMEM((SLOTS, ROWS, N), BF16),
            pltpu.VMEM((SLOTS, N, N), BF16),
            pltpu.VMEM((SLOTS, 2 * ROWS, N), BF16),
            *[pltpu.VMEM((GRP, n * SLOTS, LEV, 2, 128), BF16) for n in (2, 1, 2)],
            *[pltpu.VMEM((n * SLOTS, DEV, 2, 128), BF16) for n in (2, 1, 2)],
            pltpu.VMEM((HALF, 2 * PART), BF16),
            pltpu.VMEM((8 * DEV, HALF), BF16),
            pltpu.VMEM((2 * DEV, NLON), BF16),
            *[pltpu.VMEM((NLON, n * 128), BF16) for n in (2, 1, 2)],
            *[pltpu.VMEM((n * SLOTS, DEV, 2, 128), BF16) for n in (2, 1, 2)],
            *[pltpu.VMEM((GRP, n * SLOTS, LEV, 2, 128), BF16) for n in (2, 1, 2)],
            pltpu.SemaphoreType.DMA((4,)),
            pltpu.SemaphoreType.DMA((moves,)),
            pltpu.SemaphoreType.DMA((moves,)),
            pltpu.SemaphoreType.DMA((moves,)),
            pltpu.SemaphoreType.REGULAR,
        ],
        compiler_params=pltpu.CompilerParams(
            collective_id=0, has_side_effects=True, vmem_limit_bytes=61 << 20
        ),
    )(
        owner_table,
        owner_table,
        spectral.reshape(SLOTS, ROWS, N),
        legendre,
    )
    return out.reshape(SLOTS, 2, FIELDS, LEV, N)


def solution(mesh):
    placed = (P(("band", "grp"), None, None, None, None), P(("band", "grp"), None, None), P())
    return jax.shard_map(
        on_device,
        mesh=mesh,
        in_specs=placed,
        out_specs=P(("band", "grp"), None, None, None, None),
        check_vma=False,
    )
```
